256 devices in a mesh: ctx: 32 (over x, z), tp: 8 (over y, core).
Axes of the slice: x: 4, y: 4, z: 8, core: 2. Of those that a mesh axis runs over, the one named last changes fastest.
Arguments:
- hidden_in: bfloat16 [8192, 3072], P('ctx', 'tp'), may hold values from -96 to 96
- norm_gain: float32 [3072], replicated, may hold values from 0.1 to 1.9
- w_query: bfloat16 [3072, 3072], P(None, 'tp'), may hold values from -1 to 1
- w_key: bfloat16 [3072, 3072], P(None, 'tp'), may hold values from -1 to 1
- w_value: bfloat16 [3072, 3072], P(None, 'tp'), may hold values from -0.109375 to 0.109375
- w_out: bfloat16 [3072, 3072], P('tp'), may hold values from -0.109375 to 0.109375
- head_gain: float32 [3072], replicated, may hold values from 0.1 to 1.9
- proj_head: bfloat16 [3072, 2048], P('tp'), may hold values from -0.109375 to 0.109375
- proj_middle: bfloat16 [3072, 512], P('tp'), may hold values from -0.109375 to 0.109375
- proj_tail: bfloat16 [3072, 128], P('tp'), may hold values from -0.109375 to 0.109375
- table_head: bfloat16 [10240, 2048], P(('tp', 'ctx')), may hold values from -64 to 64
- table_middle: bfloat16 [20480, 512], P(('tp', 'ctx')), may hold values from -64 to 64
- table_tail: bfloat16 [104448, 128], P(('tp', 'ctx')), may hold values from -64 to 64
- clusters: bfloat16 [2, 2048], replicated, may hold values from -0.375 to 0.375
- targets: int32 [8192], P('ctx'), may hold values from 0 to 135167
Outputs:
- hidden_out: bfloat16 [8192, 3072], P('ctx', 'tp')
- losses: float32 [8192], P('ctx')
The draws below stay inside these ranges and needn't reach their ends.
All inputs are finite; a program needn't handle non-finite values.
Results may differ from the reference program's by a relative error of at most 0.004.
Values may be sent and summed in bfloat16 or wider, within the bound.
No kernel may reach another device: no remote copies, remote signals or barrier semaphores. Data moves between devices by JAX's collectives and lax.ppermute only.
A program may use at most 128 MiB of HBM per device.

```python
import math
import jax
import jax.numpy as jnp
import numpy as np
from jax import lax

D = 3072
HEADS = 32
HD = 96
P0 = 2048
P1 = 512
P2 = 128
V0 = 10240
V1 = 20480
V2 = 104448
SEG = 256
VOCAB = 135168
TOKENS = 8192
N_CTX = 32
N_TP = 8


def draw_hidden_in(key, part):
    base_key = jax.random.fold_in(key, 6101)
    feature_pos = jnp.arange(D, dtype=jnp.float32) / (D - 1)
    rough = jnp.exp(jax.random.uniform(jax.random.fold_in(base_key, 1), (D,), jnp.float32, math.log(0.7), math.log(1.4)))
    entries = jnp.clip(jax.random.normal(jax.random.fold_in(base_key, 2), (TOKENS, D), jnp.float32), -6.0, 6.0)
    ramp = jnp.exp(feature_pos * math.log(6.0)) * rough
    values = entries * ramp[None, :]
    return jnp.clip(values, -96.0, 96.0).astype(jnp.bfloat16)


def attention_pair(key):
    base_key = jax.random.fold_in(key, 7101)
    query_part = jax.random.normal(jax.random.fold_in(base_key, 1), (D, HEADS * HD), jnp.float32) * D ** (-0.5)
    key_part = jax.random.normal(jax.random.fold_in(base_key, 2), (D, HEADS * HD), jnp.float32) * D ** (-0.5)
    return (jnp.clip(query_part, -1.0, 1.0), jnp.clip(key_part, -1.0, 1.0))


def draw_w_query(key, part):
    return attention_pair(key)[0].astype(jnp.bfloat16)


def draw_w_key(key, part):
    return attention_pair(key)[1].astype(jnp.bfloat16)


def band_table(key, salt, row_total, table_width):
    table_key = jax.random.fold_in(key, salt)
    entries = jax.random.normal(jax.random.fold_in(table_key, 1), (row_total, table_width), jnp.float32) * (3.0 / math.sqrt(table_width))
    return jnp.clip(entries, -64.0, 64.0).astype(jnp.bfloat16)


def draw_table_head(key, part):
    return band_table(key, 8101, V0, P0)


def draw_table_middle(key, part):
    return band_table(key, 8102, V1, P1)


def draw_table_tail(key, part):
    return band_table(key, 8103, V2, P2)


def place_ends(array, stream_key, least, high):
    extent = array.shape
    place = [jax.random.randint(jax.random.fold_in(stream_key, axis), (), 0, extent[axis]) for axis in range(len(extent))]
    array = array.at[tuple(place)].set(least)
    longest = extent.index(max(extent))
    place[longest] = (place[longest] + 1) % extent[longest]
    return array.at[tuple(place)].set(high)


def block_levels(key, extent, split, least, high):
    factor_of = 1.0
    for position, parts in split:
        heights = jax.random.uniform(jax.random.fold_in(jax.random.fold_in(key, 6), position), (parts,), jnp.float32, least / len(split), high / len(split))
        factor_of = factor_of * jnp.repeat(jnp.exp(heights), extent[position] // parts).reshape((-1,) + (1,) * (len(extent) - 1 - position))
    return factor_of


def skewed_wide(key, extent, number_of, slope):
    loads = [min(1 << octave, number_of + 1 - (1 << octave)) * (1 << 20) // math.isqrt((1 << octave) ** slope) + 1 for octave in range((number_of + 1).bit_length()) if 1 << octave <= number_of]
    deviation = 1 + sum(loads) // (1 << 30)
    table = np.cumsum(np.array([max(1, weight // deviation) for weight in loads]))
    pick = jax.random.randint(jax.random.fold_in(key, 1), extent, 0, int(table[len(loads) - 1]))
    start = jnp.left_shift(1, jnp.searchsorted(jnp.asarray(table, jnp.int32), pick, side="right").astype(jnp.int32))
    rank = start - 1 + jax.random.randint(jax.random.fold_in(key, 4), extent, 0, 1 << 30) % jnp.minimum(start, number_of + 1 - start)
    return jax.random.permutation(jax.random.fold_in(key, 2), number_of)[rank].astype(jnp.int32)


def normal_values(rng, shape, scale, limit, split=(), kind=jnp.bfloat16):
    values = jax.random.normal(rng, shape, jnp.float32) * scale
    if len(split) > 0:
        values = block_levels(rng, shape, split, -0.22, 0.18) * values
    return jnp.clip(values, min=-limit, max=limit).astype(kind)


def setup_inputs(seed: int = 0) -> dict:
    keys = jax.random.split(jax.random.key(seed), 16)
    hidden_in = draw_hidden_in(jax.random.fold_in(keys[15], 71), 0)
    norm_gain = jnp.clip(1.0 + 0.18 * jax.random.normal(keys[1], (D,), jnp.float32), 0.1, 1.9)
    w_query = draw_w_query(jax.random.fold_in(keys[15], 71), 0)
    w_key = draw_w_key(jax.random.fold_in(keys[15], 71), 0)
    w_value = normal_values(keys[4], (D, HEADS * HD), D ** -0.5, 0.109375, ((1, 8),))
    w_out = normal_values(keys[5], (HEADS * HD, D), (HEADS * HD) ** -0.5, 0.109375, ((0, 8),))
    head_gain = jnp.clip(1.0 + 0.18 * jax.random.normal(keys[6], (D,), jnp.float32), 0.1, 1.9)
    proj_head = normal_values(keys[7], (D, P0), D ** -0.5, 0.109375, ((0, 8),))
    proj_middle = normal_values(keys[8], (D, P1), D ** -0.5, 0.109375, ((0, 8),))
    proj_tail = normal_values(keys[9], (D, P2), D ** -0.5, 0.109375, ((0, 8),))
    table_head = draw_table_head(jax.random.fold_in(keys[15], 71), 0)
    table_middle = draw_table_middle(jax.random.fold_in(keys[15], 71), 0)
    table_tail = draw_table_tail(jax.random.fold_in(keys[15], 71), 0)
    clusters = normal_values(keys[13], (2, P0), (P0 // 9) ** -0.5, 0.375)
    targets = place_ends(skewed_wide(keys[14], (TOKENS,), VOCAB, 2), jax.random.fold_in(keys[14], 3), 0, VOCAB - 1).astype(jnp.int32)
    return {"hidden_in": hidden_in, "norm_gain": norm_gain, "w_query": w_query, "w_key": w_key, "w_value": w_value, "w_out": w_out, "head_gain": head_gain, "proj_head": proj_head, "proj_middle": proj_middle, "proj_tail": proj_tail, "table_head": table_head, "table_middle": table_middle, "table_tail": table_tail, "clusters": clusters, "targets": targets}


def norm_rows(row_values, gain_vector):
    mean_sq = lax.optimization_barrier(jnp.mean(row_values * row_values, axis=1, keepdims=True))
    return row_values * lax.rsqrt(mean_sq + 1e-06) * gain_vector

def grouped_product(left_side, right_side, group_count):
    group_width = left_side.shape[1] // group_count
    result = jnp.zeros((left_side.shape[0], right_side.shape[1]), jnp.float32)
    for group_idx in range(group_count):
        lower = group_idx * group_width
        partial_term = jnp.dot(left_side[:, lower:lower + group_width], right_side[lower:lower + group_width], preferred_element_type=jnp.float32)
        rounded = lax.optimization_barrier(partial_term.astype(jnp.bfloat16))
        result = result + rounded.astype(jnp.float32)
    return result

def reference(hidden_in, norm_gain, w_query, w_key, w_value, w_out, head_gain, proj_head, proj_middle, proj_tail, table_head, table_middle, table_tail, clusters, targets):
    width_all = HEADS * HD
    inputs32 = hidden_in.astype(jnp.float32)
    normed = norm_rows(inputs32, norm_gain).astype(jnp.bfloat16)
    queries = jnp.dot(normed, w_query, preferred_element_type=jnp.float32).astype(jnp.bfloat16)
    key_all = jnp.dot(normed, w_key, preferred_element_type=jnp.float32).astype(jnp.bfloat16)
    value_all = jnp.dot(normed, w_value, preferred_element_type=jnp.float32).astype(jnp.bfloat16)
    padded_keys = jnp.concatenate([jnp.zeros((SEG, width_all), jnp.bfloat16), key_all], 0)
    padded_values = jnp.concatenate([jnp.zeros((SEG, width_all), jnp.bfloat16), value_all], 0)

    def segment_context(segment):
        row_start = (segment * SEG).astype(jnp.int32)
        query_rows = lax.dynamic_slice_in_dim(queries, row_start, SEG, 0).reshape(SEG, HEADS, HD).astype(jnp.float32)
        key_rows = lax.dynamic_slice_in_dim(padded_keys, row_start, 2 * SEG, 0).reshape(2 * SEG, HEADS, HD).astype(jnp.float32)
        value_rows = lax.dynamic_slice_in_dim(padded_values, row_start, 2 * SEG, 0).reshape(2 * SEG, HEADS, HD).astype(jnp.float32)
        scores = jnp.einsum('qhe,khe->hqk', query_rows, key_rows) * HD ** (-0.5)
        row_pos = lax.broadcasted_iota(jnp.int32, (SEG, 2 * SEG), 0)
        col_pos = lax.broadcasted_iota(jnp.int32, (SEG, 2 * SEG), 1)
        allowed = jnp.where(col_pos < SEG, segment > 0, col_pos - SEG <= row_pos)
        scores = jnp.where(allowed[None], scores, -1e+30)
        top_score = lax.optimization_barrier(jnp.max(scores, axis=2, keepdims=True))
        raised = jnp.exp(scores - top_score)
        weights = (raised / lax.optimization_barrier(jnp.sum(raised, axis=2, keepdims=True))).astype(jnp.bfloat16)
        mixed_rows = jnp.einsum('hqk,khe->qhe', weights.astype(jnp.float32), value_rows)
        return mixed_rows.astype(jnp.bfloat16).reshape(SEG, width_all)
    segment_ids = jnp.arange(N_CTX, dtype=jnp.int32)
    context = lax.map(segment_context, segment_ids).reshape(SEG * N_CTX, width_all)
    attention = grouped_product(context, w_out, N_TP)
    summed = inputs32 + attention
    hidden_out = summed.astype(jnp.bfloat16)
    normed_out = norm_rows(summed, head_gain).astype(jnp.bfloat16)
    band_head = grouped_product(normed_out, proj_head, N_TP).astype(jnp.bfloat16)
    band_middle = grouped_product(normed_out, proj_middle, N_TP).astype(jnp.bfloat16)
    band_tail = grouped_product(normed_out, proj_tail, N_TP).astype(jnp.bfloat16)

    def segment_loss(segment):
        row_start = (segment * SEG).astype(jnp.int32)
        head_rows = lax.dynamic_slice_in_dim(band_head, row_start, SEG, 0)
        middle_rows = lax.dynamic_slice_in_dim(band_middle, row_start, SEG, 0)
        tail_rows = lax.dynamic_slice_in_dim(band_tail, row_start, SEG, 0)
        goal = lax.dynamic_slice_in_dim(targets, row_start, SEG, 0)
        words = jnp.dot(head_rows, table_head.T, preferred_element_type=jnp.float32)
        cluster_logits = jnp.dot(head_rows, clusters.T, preferred_element_type=jnp.float32)
        head_total = jax.nn.logsumexp(jnp.concatenate([words, cluster_logits], 1), axis=1)
        middle_logits = jnp.dot(middle_rows, table_middle.T, preferred_element_type=jnp.float32)
        middle_total = jax.nn.logsumexp(middle_logits, axis=1)
        tail_logits = jnp.dot(tail_rows, table_tail.T, preferred_element_type=jnp.float32)
        tail_total = jax.nn.logsumexp(tail_logits, axis=1)
        pick_head = jnp.take_along_axis(words, jnp.clip(goal, 0, V0 - 1)[:, None], 1)[:, 0]
        pick_middle = jnp.take_along_axis(middle_logits, jnp.clip(goal - V0, 0, V1 - 1)[:, None], 1)[:, 0]
        pick_tail = jnp.take_along_axis(tail_logits, jnp.clip(goal - V0 - V1, 0, V2 - 1)[:, None], 1)[:, 0]
        loss_head = head_total - pick_head
        loss_middle = head_total - cluster_logits[:, 0] + middle_total - pick_middle
        loss_tail = head_total - cluster_logits[:, 1] + tail_total - pick_tail
        return jnp.where(goal < V0, loss_head, jnp.where(goal < V0 + V1, loss_middle, loss_tail))
    losses = lax.map(segment_loss, segment_ids).reshape(SEG * N_CTX)
    return (hidden_out, losses)
```

```python
import jax
import jax.numpy as jnp
from jax import lax
from jax.experimental import pallas as pl
from jax.experimental.pallas import tpu as pltpu
from jax.sharding import Mesh
from jax.sharding import PartitionSpec as P


D = 3072
HD = 96
V0 = 10240
V1 = 20480
V2 = 104448
P0 = 2048
P1 = 512
P2 = 128
SEG = 256
N_TP = 8
N_CTX = 32
LW = D // N_TP
TOK = SEG // N_TP
BAND = P0 + P1 + P2
WIDE = BAND + 128
HEAD_ROWS = V0 // 256
MID_ROWS = V1 // 256
TAIL_ROWS = V2 // 256
PACK_HEAD = HEAD_ROWS * P0 // 256
PACK_MID = MID_ROWS * P1 // 256
TAIL_LEFT = 208
TAIL_RIGHT = TAIL_ROWS - TAIL_LEFT
PACK_ROWS = PACK_HEAD + PACK_MID + TAIL_LEFT
NEG_FILL = -1e30
CTX = ("xh", "xl", "z")
TP = ("y", "core")
F32 = jnp.float32
BF16 = jnp.bfloat16


VMEM_SPEC = pl.BlockSpec(memory_space=pltpu.VMEM)
ANY_SPEC = pl.BlockSpec(memory_space=pl.ANY)
SMEM_SPEC = pl.BlockSpec(memory_space=pltpu.SMEM)


def route(step_y, flip):
    return [
        (2 * y + core, 2 * ((y + step_y) % 4) + (core ^ flip)) for y in range(4) for core in range(2)
    ]


def to_y(block, step_y):
    return lax.ppermute(block, TP, route(step_y, 0))


def to_partner(block):
    return lax.ppermute(block, TP, route(0, 1))


def to_mate(block):
    return lax.ppermute(
        block, CTX, [(8 * x + z, 8 * (x ^ 2) + z) for x in range(4) for z in range(8)]
    )


def from_y(block):
    return [block] + [to_y(block, d) for d in (1, 2, 3)]


def source_of(place, d, flip):
    y, core = place // 2, place % 2
    return 2 * lax.rem(y - d + 4, 4) + (core + flip) % 2


def target_of(place, d, flip):
    y, core = place // 2, place % 2
    return 2 * lax.rem(y + d, 4) + (core + flip) % 2


def vmem_params(mib):
    return pltpu.CompilerParams(vmem_limit_bytes=mib * 1024 * 1024)


def products(place, refs, entries, gain_ref, weights, totals, square):
    for ref, (d, flip) in zip(refs, entries):
        src = source_of(place, d, flip)
        part = ref[...].astype(F32)
        square = square + jnp.sum(part * part, axis=1, keepdims=True)
        scaled = (part * gain_ref[pl.ds(src, 1), :]).astype(BF16)
        rows = pl.ds(pl.multiple_of(src * LW, LW), LW)
        for i, w_ref in enumerate(weights):
            got = jnp.dot(scaled, w_ref[rows, :], preferred_element_type=F32)
            totals[i] = got if totals[i] is None else totals[i] + got
    return totals, square


NEAR = ((0, 0), (0, 1))
FAR = ((1, 0), (1, 1), (3, 0), (3, 1), (2, 0), (2, 1))


def near_kernel(place_ref, gain_ref, wq_ref, wk_ref, wv_ref, a_ref, b_ref, part_ref, square_ref):
    totals, square = products(
        place_ref[0], (a_ref, b_ref), NEAR, gain_ref, (wq_ref, wk_ref, wv_ref), [None] * 3,
        jnp.zeros((SEG, 1), F32),
    )
    for i, total in enumerate(totals):
        part_ref[:, i * LW : (i + 1) * LW] = total
    square_ref[...] = jnp.broadcast_to(square, (SEG, 128))


def far_kernel(place_ref, gain_ref, wq_ref, wk_ref, wv_ref, part_ref, square_ref, *refs):
    q_ref, kv_ref = refs[6:]
    totals, square = products(
        place_ref[0], refs[:6], FAR, gain_ref, (wq_ref, wk_ref, wv_ref),
        [part_ref[:, i * LW : (i + 1) * LW] for i in range(3)], square_ref[:, 0:1],
    )
    scale = lax.rsqrt(square / D + 1e-06)
    q_ref[...] = (totals[0] * scale).astype(BF16)
    kv_ref[:, 0:LW] = (totals[1] * scale).astype(BF16)
    kv_ref[:, LW : 2 * LW] = (totals[2] * scale).astype(BF16)


def qkv_near(place, gain, weights, blocks):
    return pl.pallas_call(
        near_kernel,
        out_shape=(
            jax.ShapeDtypeStruct((SEG, 3 * LW), F32),
            jax.ShapeDtypeStruct((SEG, 128), F32),
        ),
        in_specs=[SMEM_SPEC] + [VMEM_SPEC] * 6,
        out_specs=(VMEM_SPEC,) * 2,
        compiler_params=vmem_params(8),
        name="qkv_near",
    )(place, gain, *weights, *blocks)


def qkv_far(place, gain, weights, near, blocks):
    return pl.pallas_call(
        far_kernel,
        out_shape=(
            jax.ShapeDtypeStruct((SEG, LW), BF16),
            jax.ShapeDtypeStruct((SEG, 2 * LW), BF16),
        ),
        in_specs=[SMEM_SPEC] + [VMEM_SPEC] * 12,
        out_specs=(VMEM_SPEC,) * 2,
        compiler_params=vmem_params(12),
        name="qkv_far",
    )(place, gain, *weights, *near, *blocks)


def attend_kernel(place_ref, q_ref, now_ref, past_ref, wo_ref, keep_ref, give_ref):
    k_ref, v_ref = now_ref.at[:, 0:LW], now_ref.at[:, LW : 2 * LW]
    km_ref, vm_ref = past_ref.at[:, 0:LW], past_ref.at[:, LW : 2 * LW]
    place = place_ref[0]
    first = place_ref[1] == 0
    row = lax.broadcasted_iota(jnp.int32, (SEG, SEG), 0)
    col = lax.broadcasted_iota(jnp.int32, (SEG, SEG), 1)
    causal = col <= row
    lane = lax.broadcasted_iota(jnp.int32, (SEG, LW), 1) // HD
    q = q_ref[...]
    nt = (((1,), (1,)), ((), ()))
    context = jnp.zeros((SEG, LW), F32)
    for h in range(LW // HD):
        mine = lane == h
        qh = jnp.where(mine, q, jnp.zeros_like(q))
        own = lax.dot_general(qh, k_ref[...], nt, preferred_element_type=F32) * HD ** (-0.5)
        old = lax.dot_general(qh, km_ref[...], nt, preferred_element_type=F32) * HD ** (-0.5)
        own = jnp.where(causal, own, NEG_FILL)
        old = jnp.where(first, NEG_FILL, old)
        top = jnp.maximum(
            jnp.max(own, axis=1, keepdims=True), jnp.max(old, axis=1, keepdims=True)
        )
        own = jnp.exp(own - top)
        old = jnp.exp(old - top)
        total = jnp.sum(own, axis=1, keepdims=True) + jnp.sum(old, axis=1, keepdims=True)
        own = (own / total).astype(BF16)
        old = (old / total).astype(BF16)
        mixed = jnp.dot(own, v_ref[...], preferred_element_type=F32) + jnp.dot(
            old, vm_ref[...], preferred_element_type=F32
        )
        context = jnp.where(mine, mixed, context)
    context = context.astype(BF16)
    for flip, out_ref in ((1, give_ref), (0, keep_ref)):
        for d in range(4):
            start = pl.multiple_of(target_of(place, d, flip) * LW, LW)
            out_ref[d] = jnp.dot(
                context, wo_ref[:, pl.ds(start, LW)], preferred_element_type=F32
            ).astype(out_ref.dtype)


def attend(place, q, now, past, wo):
    return pl.pallas_call(
        attend_kernel,
        out_shape=(
            jax.ShapeDtypeStruct((4, SEG, LW), F32),
            jax.ShapeDtypeStruct((4, SEG, LW), BF16),
        ),
        in_specs=[SMEM_SPEC] + [VMEM_SPEC] * 4,
        out_specs=(VMEM_SPEC,) * 2,
        compiler_params=vmem_params(12),
        name="attend",
    )(place, q, now, past, wo)


def pair_kernel(keep_ref, got_ref, mine_ref, *out_refs):
    mine_ref[...] = keep_ref[0] + got_ref[0].astype(F32)
    for d in (1, 2, 3):
        out_refs[d - 1][...] = (keep_ref[d] + got_ref[d].astype(F32)).astype(BF16)


def pair(keep, got):
    shape = keep.shape[1:]
    return pl.pallas_call(
        pair_kernel,
        out_shape=(jax.ShapeDtypeStruct(shape, F32),) + (jax.ShapeDtypeStruct(shape, BF16),) * 3,
        in_specs=[VMEM_SPEC] * 2,
        out_specs=(VMEM_SPEC,) * 4,
        compiler_params=vmem_params(3),
        name="pair",
    )(keep, got)


def split_square(square):
    high = square.astype(BF16)
    low = (square - high.astype(F32)).astype(BF16)
    lane = lax.broadcasted_iota(jnp.int32, (square.shape[0], 128), 1)
    return jnp.where(
        lane == 0, high.astype(F32), jnp.where(lane == 1, low.astype(F32), 0.0)
    )


def project_kernel(
    place_ref, gain_ref, x_ref, a0_ref, a1_ref, a2_ref, a3_ref, ph_ref, pm_ref, pt_ref,
    hidden_ref, keep_ref, give_ref, part_ref,
):
    place = place_ref[0]
    attention = a0_ref[...]
    for ref in (a1_ref, a2_ref, a3_ref):
        attention = attention + ref[...].astype(F32)
    summed = x_ref[...].astype(F32) + attention
    hidden_ref[...] = summed.astype(BF16)
    square = jnp.sum(summed * summed, axis=1, keepdims=True)
    scaled = (summed * gain_ref[pl.ds(place, 1), :]).astype(BF16)
    part_ref[:, 0:P0] = jnp.dot(scaled, ph_ref[...], preferred_element_type=F32)
    part_ref[:, P0 : P0 + P1] = jnp.dot(scaled, pm_ref[...], preferred_element_type=F32)
    part_ref[:, P0 + P1 : BAND] = jnp.dot(scaled, pt_ref[...], preferred_element_type=F32)
    part_ref[:, BAND:WIDE] = split_square(square)
    for d in range(4):
        rows = pl.ds(pl.multiple_of(target_of(place, d, 1) * TOK, TOK), TOK)
        give_ref[d] = part_ref[rows, :].astype(BF16)
        rows = pl.ds(pl.multiple_of(target_of(place, d, 0) * TOK, TOK), TOK)
        keep_ref[d] = part_ref[rows, :]


def project(place, gain, x, parts, ph, pm, pt):
    return pl.pallas_call(
        project_kernel,
        out_shape=(
            jax.ShapeDtypeStruct((SEG, LW), BF16),
            jax.ShapeDtypeStruct((4, TOK, WIDE), F32),
            jax.ShapeDtypeStruct((4, TOK, WIDE), BF16),
        ),
        in_specs=[SMEM_SPEC] + [VMEM_SPEC] * 9,
        out_specs=(VMEM_SPEC,) * 3,
        scratch_shapes=[pltpu.VMEM((SEG, WIDE), F32)],
        compiler_params=vmem_params(12),
        name="project",
    )(place, gain, x, *parts, ph, pm, pt)


def pair_band_kernel(keep_ref, got_ref, mine_ref, *out_refs):
    for d in range(4):
        band = keep_ref[d, :, 0:BAND] + got_ref[d, :, 0:BAND].astype(F32)
        tail = keep_ref[d, :, BAND:WIDE] + got_ref[d, :, BAND:WIDE].astype(F32)
        if d == 0:
            mine_ref[:, 0:BAND] = band
            mine_ref[:, BAND:WIDE] = tail
        else:
            square = tail[:, 0:1] + tail[:, 1:2]
            out_refs[d - 1][:, 0:BAND] = band.astype(BF16)
            out_refs[d - 1][:, BAND:WIDE] = split_square(square).astype(BF16)


def pair_band(keep, got):
    shape = keep.shape[1:]
    return pl.pallas_call(
        pair_band_kernel,
        out_shape=(jax.ShapeDtypeStruct(shape, F32),) + (jax.ShapeDtypeStruct(shape, BF16),) * 3,
        in_specs=[VMEM_SPEC] * 2,
        out_specs=(VMEM_SPEC,) * 4,
        compiler_params=vmem_params(3),
        name="pair_band",
    )(keep, got)


def finish_band_kernel(place_ref, info_ref, a0_ref, a1_ref, a2_ref, a3_ref, out_ref):
    total = a0_ref[...]
    for ref in (a1_ref, a2_ref, a3_ref):
        total = total + ref[...].astype(F32)
    square = total[:, BAND : BAND + 1] + total[:, BAND + 1 : BAND + 2]
    out_ref[:, 0:BAND] = (total[:, 0:BAND] * lax.rsqrt(square / D + 1e-06)).astype(BF16)
    out_ref[:, BAND:WIDE] = info_ref[pl.ds(pl.multiple_of(place_ref[0] * TOK, TOK), TOK), :]


def finish_band(place, info, parts):
    return pl.pallas_call(
        finish_band_kernel,
        out_shape=jax.ShapeDtypeStruct((TOK, WIDE), BF16),
        in_specs=[SMEM_SPEC] + [VMEM_SPEC] * 5,
        out_specs=VMEM_SPEC,
        compiler_params=vmem_params(3),
        name="finish_band",
    )(place, info, *parts)


def target_info(targets):
    band = (targets >= V0).astype(jnp.int32) + (targets >= V0 + V1).astype(jnp.int32)
    code, row = jnp.zeros_like(targets), jnp.zeros_like(targets)
    for b, (first, rows) in enumerate(((0, HEAD_ROWS), (V0, MID_ROWS), (V0 + V1, TAIL_ROWS))):
        word = jnp.maximum(targets - first, 0)
        shard, within = word // rows, word % rows
        there, place = shard // N_CTX, shard % N_CTX
        code = jnp.where(band == b, 8 * b + there // 2 * 2 + place // 16, code)
        row = jnp.where(band == b, (place % 16 * 2 + there % 2) * rows + within, row)
    columns = jnp.stack([code, row // 256, row % 256], 1)
    return jnp.pad(columns, ((0, 0), (0, 125))).astype(BF16)


def turn_kernel(place_ref, clus_ref, *refs):
    blocks = refs[:8]
    flip_ref, cl_ref, goal_ref, rows_ref = refs[8:]
    y, half = place_ref[0] // 2, place_ref[1] // 16
    for j, ref in enumerate(blocks):
        src = lax.rem(y - j // 2 + 4, 4) + 4 * ((half + j) % 2)
        rows_ref[pl.ds(pl.multiple_of(src * TOK, TOK), TOK), :] = ref[...]
    flip_ref[...] = rows_ref[...].T
    cl_ref[...] = jnp.dot(clus_ref[...], flip_ref[0:P0, :], preferred_element_type=F32)
    info = flip_ref[BAND : BAND + 16, :].astype(F32)
    code = info[0:1].astype(jnp.int32)
    row = (info[1:2] * 256.0 + info[2:3]).astype(jnp.int32)
    goals = [jnp.where(code == 8 * b + 2 * y + half, row, -(1 << 24)) for b in range(3)]
    kind = (code >= 8).astype(jnp.int32) + (code >= 16).astype(jnp.int32)
    goal_ref[...] = jnp.concatenate(goals + [kind] * 5, 0)


def turned(place, clusters, blocks):
    return pl.pallas_call(
        turn_kernel,
        out_shape=(
            jax.ShapeDtypeStruct((WIDE, SEG), BF16),
            jax.ShapeDtypeStruct((2, SEG), F32),
            jax.ShapeDtypeStruct((8, SEG), jnp.int32),
        ),
        in_specs=[SMEM_SPEC] + [VMEM_SPEC] * 9,
        out_specs=(VMEM_SPEC,) * 3,
        scratch_shapes=[pltpu.VMEM((SEG, WIDE), BF16)],
        compiler_params=vmem_params(6),
        name="turned",
    )(place, clusters, *blocks)


def unpack_kernel(table_ref, head_ref, mid_ref, tail_ref, sem):
    def one(s, carry):
        for j in range(P0 // 256):
            to = pl.ds(pl.multiple_of(s * HEAD_ROWS, 8), HEAD_ROWS)
            pltpu.make_async_copy(
                table_ref.at[s, pl.ds(j * HEAD_ROWS, HEAD_ROWS), :],
                head_ref.at[to, pl.ds(j * 256, 256)], sem.at[0],
            ).start()
        for j in range(P1 // 256):
            to = pl.ds(pl.multiple_of(s * MID_ROWS, 8), MID_ROWS)
            pltpu.make_async_copy(
                table_ref.at[s, pl.ds(PACK_HEAD + j * MID_ROWS, MID_ROWS), :],
                mid_ref.at[to, pl.ds(j * 256, 256)], sem.at[1],
            ).start()
        for j, (offset, rows) in enumerate(((0, TAIL_LEFT), (TAIL_LEFT, TAIL_RIGHT))):
            to = pl.ds(pl.multiple_of(s * TAIL_ROWS + offset, 8), rows)
            pltpu.make_async_copy(
                table_ref.at[s, pl.ds(PACK_HEAD + PACK_MID, rows), pl.ds(j * 128, 128)],
                tail_ref.at[to, :], sem.at[2],
            ).start()
        return carry

    lax.fori_loop(0, N_CTX, one, 0)
    for k, ref in enumerate((head_ref, mid_ref, tail_ref)):
        pltpu.make_async_copy(ref, ref, sem.at[k]).wait()


def unpacked(table):
    return pl.pallas_call(
        unpack_kernel,
        out_shape=(
            jax.ShapeDtypeStruct((HEAD_ROWS * N_CTX, P0), BF16),
            jax.ShapeDtypeStruct((MID_ROWS * N_CTX, P1), BF16),
            jax.ShapeDtypeStruct((TAIL_ROWS * N_CTX, P2), BF16),
        ),
        in_specs=[ANY_SPEC],
        out_specs=(VMEM_SPEC,) * 3,
        scratch_shapes=[pltpu.SemaphoreType.DMA((3,))],
        compiler_params=vmem_params(40),
        name="unpacked",
    )(table)


LOG2_E = 1.4426950408889634
LANES = 2


def fold(words_ref, flip_ref, even_ref, odd_ref, first, width, total, goal, rows):
    near = goal - lax.broadcasted_iota(jnp.int32, (8, SEG), 0)
    flip = flip_ref.at[first : first + width, :]
    count = total // rows

    def load(i, store_ref):
        start = pl.multiple_of(i * rows, rows)
        logits = jnp.dot(
            words_ref[pl.ds(start, rows), :], flip[...], preferred_element_type=F32
        )
        store_ref[0:rows, :] = logits
        return jnp.max(logits.reshape(rows // 8, 8, SEG), axis=0)

    def use(i, store_ref, highest, state):
        top, acc, pick = state
        new_top = jnp.maximum(top, highest)
        shift = new_top * LOG2_E
        sums = [acc * jnp.exp2(top * LOG2_E - shift)] + [jnp.zeros((8, SEG), F32)] * (LANES - 1)
        picks = [pick] + [jnp.zeros((8, SEG), F32)] * (LANES - 1)
        here = near - i * rows
        for r in range(rows // 8):
            part = store_ref[8 * r : 8 * r + 8, :]
            k = r % LANES
            sums[k] = sums[k] + jnp.exp2(part * LOG2_E - shift)
            picks[k] = jnp.where(here == 8 * r, part, picks[k])
        return new_top, sum(sums[1:], sums[0]), sum(picks[1:], picks[0])

    def step(i, carry):
        state, highest = carry
        following = load(2 * i + 1, odd_ref)
        state = use(2 * i, even_ref, highest, state)
        highest = load(jnp.minimum(2 * i + 2, count - 1), even_ref)
        state = use(2 * i + 1, odd_ref, following, state)
        return state, highest

    empty = (
        jnp.full((8, SEG), NEG_FILL, F32),
        jnp.zeros((8, SEG), F32),
        jnp.zeros((8, SEG), F32),
    )
    (top, acc, pick), _ = lax.fori_loop(0, count // 2, step, (empty, load(0, even_ref)))
    highest = jnp.max(top, axis=0, keepdims=True)
    total_exp = jnp.sum(acc * jnp.exp(top - highest), axis=0, keepdims=True)
    return highest, total_exp, jnp.sum(pick, axis=0, keepdims=True)


def words_kernel(goal_ref, flip_ref, head_ref, mid_ref, tail_ref, out_ref, even_ref, odd_ref):
    refs = (flip_ref, even_ref, odd_ref)
    n0, n1, n2 = HEAD_ROWS * N_CTX, MID_ROWS * N_CTX, TAIL_ROWS * N_CTX
    m = fold(mid_ref, *refs, P0, P1, n1, goal_ref[1:2, :], 256)
    t = fold(tail_ref, *refs, P0 + P1, P2, n2, goal_ref[2:3, :], 384)
    h = fold(head_ref, *refs, 0, P0, n0, goal_ref[0:1, :], 320)
    out_ref[...] = jnp.concatenate(
        [h[0], h[1], m[0], m[1], t[0], t[1], h[2] + m[2] + t[2], jnp.zeros((1, SEG), F32)], 0
    )


def words(goals, flip, tables):
    return pl.pallas_call(
        words_kernel,
        out_shape=jax.ShapeDtypeStruct((8, SEG), F32),
        in_specs=[VMEM_SPEC] * 5,
        out_specs=VMEM_SPEC,
        scratch_shapes=[pltpu.VMEM((384, SEG), F32), pltpu.VMEM((384, SEG), F32)],
        compiler_params=vmem_params(6),
        name="words",
    )(goals, flip, *tables)


def join(one, other):
    rows = []
    for b in range(3):
        top = jnp.maximum(one[2 * b : 2 * b + 1], other[2 * b : 2 * b + 1])
        rows += [
            top,
            one[2 * b + 1 : 2 * b + 2] * jnp.exp(one[2 * b : 2 * b + 1] - top)
            + other[2 * b + 1 : 2 * b + 2] * jnp.exp(other[2 * b : 2 * b + 1] - top),
        ]
    return jnp.concatenate(rows + [one[6:7] + other[6:7], jnp.zeros((1, SEG), F32)], 0)


def join_kernel(a_ref, b_ref, out_ref):
    out_ref[...] = join(a_ref[...], b_ref[...])


def loss_kernel(place_ref, goal_ref, cl_ref, a_ref, b_ref, c_ref, d_ref, out_ref):
    stats = join(join(a_ref[...], b_ref[...]), join(c_ref[...], d_ref[...]))
    kind = goal_ref[3:4, :]
    c0, c1 = cl_ref[0:1, :], cl_ref[1:2, :]
    word_total = stats[0:1] + jnp.log(stats[1:2])
    top = jnp.maximum(word_total, jnp.maximum(c0, c1))
    head_total = top + jnp.log(
        jnp.exp(word_total - top) + jnp.exp(c0 - top) + jnp.exp(c1 - top)
    )
    mid_total = stats[2:3] + jnp.log(stats[3:4])
    tail_total = stats[4:5] + jnp.log(stats[5:6])
    pick = stats[6:7]
    losses = jnp.where(
        kind == 0,
        head_total - pick,
        jnp.where(
            kind == 1,
            head_total - c0 + mid_total - pick,
            head_total - c1 + tail_total - pick,
        ),
    )
    losses = jnp.where(place_ref[1] < 16, losses[:, 0:128], losses[:, 128:256])
    out_ref[...] = jnp.broadcast_to(losses, (8, 128))


def order_kernel(place_ref, mine_ref, other_ref, out_ref):
    core = place_ref[0] % 2
    for y in range(4):
        for flip, ref in ((0, mine_ref), (1, other_ref)):
            rows = pltpu.roll(ref[...], (128 - y * TOK) % 128, 1) if y else ref[...]
            out_ref[pl.ds(2 * y + (core + flip) % 2, 1), :] = rows[0:1]


def ordered(place, mine, other):
    return pl.pallas_call(
        order_kernel,
        out_shape=jax.ShapeDtypeStruct((8, 128), F32),
        in_specs=[SMEM_SPEC] + [VMEM_SPEC] * 2,
        out_specs=VMEM_SPEC,
        compiler_params=vmem_params(1),
        name="ordered",
    )(place, mine, other)


def joined(one, other):
    return pl.pallas_call(
        join_kernel,
        out_shape=jax.ShapeDtypeStruct((8, SEG), F32),
        in_specs=[VMEM_SPEC] * 2,
        out_specs=VMEM_SPEC,
        compiler_params=vmem_params(1),
        name="joined",
    )(one, other)


def loss(place, goals, cl, stats):
    return pl.pallas_call(
        loss_kernel,
        out_shape=jax.ShapeDtypeStruct((8, 128), F32),
        in_specs=[SMEM_SPEC] + [VMEM_SPEC] * 6,
        out_specs=VMEM_SPEC,
        compiler_params=vmem_params(1),
        name="loss",
    )(place, goals, cl, *stats)


def pack_kernel(head_ref, mid_ref, tail_ref, out_ref, sem):
    copies = []
    for j in range(P0 // 256):
        copies.append((head_ref.at[:, pl.ds(j * 256, 256)], j * HEAD_ROWS, HEAD_ROWS, 0, 256))
    for j in range(P1 // 256):
        start = PACK_HEAD + j * MID_ROWS
        copies.append((mid_ref.at[:, pl.ds(j * 256, 256)], start, MID_ROWS, 0, 256))
    start = PACK_HEAD + PACK_MID
    copies.append((tail_ref.at[pl.ds(0, TAIL_LEFT), :], start, TAIL_LEFT, 0, 128))
    copies.append((tail_ref.at[pl.ds(TAIL_LEFT, TAIL_RIGHT), :], start, TAIL_RIGHT, 128, 128))
    under = TAIL_LEFT - TAIL_RIGHT
    copies.append((tail_ref.at[pl.ds(0, under), :], start + TAIL_RIGHT, under, 128, 128))
    moves = [
        pltpu.make_async_copy(
            source, out_ref.at[pl.ds(row, rows), pl.ds(col, cols)], sem.at[i]
        )
        for i, (source, row, rows, col, cols) in enumerate(copies)
    ]
    for move in moves:
        move.start()
    for move in moves:
        move.wait()


def packed_tables(table_head, table_middle, table_tail):
    return pl.pallas_call(
        pack_kernel,
        out_shape=jax.ShapeDtypeStruct((PACK_ROWS, 256), BF16),
        in_specs=[ANY_SPEC] * 3,
        out_specs=ANY_SPEC,
        scratch_shapes=[pltpu.SemaphoreType.DMA((P0 // 256 + P1 // 256 + 3,))],
        compiler_params=vmem_params(1),
        name="packed",
    )(table_head, table_middle, table_tail)


def layer(
    hidden_in, norm_gain, w_query, w_key, w_value, w_out, head_gain,
    proj_head, proj_middle, proj_tail, table_head, table_middle, table_tail, clusters, targets,
):
    tp_rank = lax.axis_index(TP)
    ctx_rank = lax.axis_index(CTX)
    place = jnp.stack([tp_rank, ctx_rank]).astype(jnp.int32)
    info = target_info(targets)
    gain = norm_gain.reshape(N_TP, LW)
    weights = (w_query, w_key, w_value)
    blocks = {}
    blocks[0, 1] = to_partner(hidden_in)
    for d in (1, 3, 2):
        blocks[d, 0] = to_y(hidden_in, d)
    blocks[0, 1], *tables = lax.optimization_barrier(
        (blocks[0, 1], table_head, table_middle, table_tail)
    )
    table = lax.all_gather(packed_tables(*tables), ("xl", "z", "core"))
    for d in (1, 3, 2):
        blocks[d, 1] = to_partner(blocks[d, 0])
    near = qkv_near(place, gain, weights, (hidden_in, blocks[0, 1]))
    q, now = qkv_far(place, gain, weights, near, [blocks[e] for e in FAR])
    past = lax.ppermute(now, CTX, [(i, i + 1) for i in range(N_CTX - 1)])
    keep, give = attend(place, q, now, past, w_out)
    mine, *others = pair(keep, to_partner(give))
    parts = [mine] + [to_y(o, d) for o, d in zip(others, (1, 2, 3))]
    hidden_out, keep, give = project(
        place, head_gain.reshape(N_TP, LW), hidden_in, parts, proj_head, proj_middle, proj_tail
    )
    mine, *others = pair_band(keep, to_partner(give))
    parts = [mine] + [to_y(o, d) for o, d in zip(others, (1, 2, 3))]
    band = finish_band(place, info, parts)
    band_x, table = lax.optimization_barrier((to_mate(band), table))
    tables = unpacked(table)
    bands = [band, band_x]
    for d in (1, 2, 3):
        bands += [to_y(band, d), to_y(band_x, d)]
    *bands, first, second, third = lax.optimization_barrier((*bands, *tables))
    flip, cl, goals = turned(place, clusters, bands)
    stats = words(goals, flip, (first, second, third))
    stats = joined(stats, to_mate(stats))
    done = loss(place, goals, cl, from_y(stats))
    losses = ordered(place, done, to_partner(done))[:, :TOK].reshape(SEG)
    return (hidden_out, losses)


def solution(mesh):
    fine = Mesh(mesh.devices.reshape(2, 2, 8, 4, 2), CTX + TP)
    placed = (
        P(CTX, TP),
        P(),
        P(None, TP),
        P(None, TP),
        P(None, TP),
        P(TP, None),
        P(),
        P(TP, None),
        P(TP, None),
        P(TP, None),
        P(TP + CTX, None),
        P(TP + CTX, None),
        P(TP + CTX, None),
        P(),
        P(CTX),
    )
    return jax.shard_map(
        layer, mesh=fine, in_specs=placed, out_specs=(P(CTX, TP), P(CTX)), check_vma=False
    )
```

```python
import jax
import jax.numpy as jnp
from jax import lax
from jax.experimental import pallas as pl
from jax.experimental.pallas import tpu as pltpu
from jax.sharding import Mesh
from jax.sharding import PartitionSpec as P


D = 3072
HD = 96
V0 = 10240
V1 = 20480
V2 = 104448
P0 = 2048
P1 = 512
P2 = 128
SEG = 256
N_TP = 8
N_CTX = 32
LW = D // N_TP
TOK = SEG // N_TP
BAND = P0 + P1 + P2
WIDE = BAND + 128
HEAD_ROWS = V0 // 256
MID_ROWS = V1 // 256
TAIL_ROWS = V2 // 256
PACK_HEAD = HEAD_ROWS * P0 // 256
PACK_MID = MID_ROWS * P1 // 256
TAIL_LEFT = 208
TAIL_RIGHT = TAIL_ROWS - TAIL_LEFT
PACK_ROWS = PACK_HEAD + PACK_MID + TAIL_LEFT
NEG_FILL = -1e30
CTX = ("xh", "xl", "z")
TP = ("y", "core")
F32 = jnp.float32
BF16 = jnp.bfloat16


VMEM_SPEC = pl.BlockSpec(memory_space=pltpu.VMEM)
ANY_SPEC = pl.BlockSpec(memory_space=pl.ANY)
SMEM_SPEC = pl.BlockSpec(memory_space=pltpu.SMEM)


def route(step_y, flip):
    return [
        (2 * y + core, 2 * ((y + step_y) % 4) + (core ^ flip)) for y in range(4) for core in range(2)
    ]


def to_y(block, step_y):
    return lax.ppermute(block, TP, route(step_y, 0))


def to_partner(block):
    return lax.ppermute(block, TP, route(0, 1))


def to_mate(block):
    return lax.ppermute(
        block, CTX, [(8 * x + z, 8 * (x ^ 2) + z) for x in range(4) for z in range(8)]
    )


def from_y(block):
    return [block] + [to_y(block, d) for d in (1, 2, 3)]


def source_of(place, d, flip):
    y, core = place // 2, place % 2
    return 2 * lax.rem(y - d + 4, 4) + (core + flip) % 2


def target_of(place, d, flip):
    y, core = place // 2, place % 2
    return 2 * lax.rem(y + d, 4) + (core + flip) % 2


def vmem_params(mib):
    return pltpu.CompilerParams(vmem_limit_bytes=mib * 1024 * 1024)


def products(place, refs, entries, gain_ref, weights, totals, square):
    for ref, (d, flip) in zip(refs, entries):
        src = source_of(place, d, flip)
        part = ref[...].astype(F32)
        square = square + jnp.sum(part * part, axis=1, keepdims=True)
        scaled = (part * gain_ref[pl.ds(src, 1), :]).astype(BF16)
        rows = pl.ds(pl.multiple_of(src * LW, LW), LW)
        for i, w_ref in enumerate(weights):
            got = jnp.dot(scaled, w_ref[rows, :], preferred_element_type=F32)
            totals[i] = got if totals[i] is None else totals[i] + got
    return totals, square


NEAR = ((0, 0), (0, 1))
FAR = ((1, 0), (1, 1), (3, 0), (3, 1), (2, 0), (2, 1))


def near_kernel(place_ref, gain_ref, wq_ref, wk_ref, wv_ref, a_ref, b_ref, part_ref, square_ref):
    totals, square = products(
        place_ref[0], (a_ref, b_ref), NEAR, gain_ref, (wq_ref, wk_ref, wv_ref), [None] * 3,
        jnp.zeros((SEG, 1), F32),
    )
    for i, total in enumerate(totals):
        part_ref[:, i * LW : (i + 1) * LW] = total
    square_ref[...] = jnp.broadcast_to(square, (SEG, 128))


def far_kernel(place_ref, gain_ref, wk_ref, wv_ref, part_ref, square_ref, *refs):
    kv_ref, scale_ref = refs[6:]
    totals, square = products(
        place_ref[0], refs[:6], FAR, gain_ref, (wk_ref, wv_ref),
        [part_ref[:, i * LW : (i + 1) * LW] for i in (1, 2)], square_ref[:, 0:1],
    )
    scale = lax.rsqrt(square / D + 1e-06)
    kv_ref[:, 0:LW] = (totals[0] * scale).astype(BF16)
    kv_ref[:, LW : 2 * LW] = (totals[1] * scale).astype(BF16)
    scale_ref[...] = jnp.broadcast_to(scale, (SEG, 128))


NT = (((1,), (1,)), ((), ()))


def own_kernel(place_ref, gain_ref, wq_ref, part_ref, scale_ref, now_ref, *refs):
    q_ref, acc_ref, stats_ref = refs[6:]
    totals, _ = products(
        place_ref[0], refs[:6], FAR, gain_ref, (wq_ref,), [part_ref[:, 0:LW]],
        jnp.zeros((SEG, 1), F32),
    )
    q = (totals[0] * scale_ref[:, 0:1]).astype(BF16)
    q_ref[...] = q
    row = lax.broadcasted_iota(jnp.int32, (SEG, SEG), 0)
    col = lax.broadcasted_iota(jnp.int32, (SEG, SEG), 1)
    causal = col <= row
    head = lax.broadcasted_iota(jnp.int32, (SEG, LW), 1) // HD
    lane = lax.broadcasted_iota(jnp.int32, (SEG, 128), 1)
    acc = jnp.zeros((SEG, LW), F32)
    stats = jnp.zeros((SEG, 128), F32)
    for h in range(LW // HD):
        qh = jnp.where(head == h, q, jnp.zeros_like(q))
        own = lax.dot_general(qh, now_ref[:, 0:LW], NT, preferred_element_type=F32) * HD ** (-0.5)
        own = jnp.where(causal, own, NEG_FILL)
        top = jnp.max(own, axis=1, keepdims=True)
        own = jnp.exp(own - top)
        stats = jnp.where(lane == h, top, stats)
        stats = jnp.where(lane == 4 + h, jnp.sum(own, axis=1, keepdims=True), stats)
        mixed = jnp.dot(own.astype(BF16), now_ref[:, LW : 2 * LW], preferred_element_type=F32)
        acc = jnp.where(head == h, mixed, acc)
    acc_ref[...] = acc
    stats_ref[...] = stats


def own_attention(place, gain, w_query, near, scale, now, blocks):
    return pl.pallas_call(
        own_kernel,
        out_shape=(
            jax.ShapeDtypeStruct((SEG, LW), BF16),
            jax.ShapeDtypeStruct((SEG, LW), F32),
            jax.ShapeDtypeStruct((SEG, 128), F32),
        ),
        in_specs=[SMEM_SPEC] + [VMEM_SPEC] * 11,
        out_specs=(VMEM_SPEC,) * 3,
        compiler_params=vmem_params(12),
        name="own_attention",
    )(place, gain, w_query, near, scale, now, *blocks)


def qkv_near(place, gain, weights, blocks):
    return pl.pallas_call(
        near_kernel,
        out_shape=(
            jax.ShapeDtypeStruct((SEG, 3 * LW), F32),
            jax.ShapeDtypeStruct((SEG, 128), F32),
        ),
        in_specs=[SMEM_SPEC] + [VMEM_SPEC] * 6,
        out_specs=(VMEM_SPEC,) * 2,
        compiler_params=vmem_params(8),
        name="qkv_near",
    )(place, gain, *weights, *blocks)


def kv_far(place, gain, weights, near, blocks):
    return pl.pallas_call(
        far_kernel,
        out_shape=(
            jax.ShapeDtypeStruct((SEG, 2 * LW), BF16),
            jax.ShapeDtypeStruct((SEG, 128), F32),
        ),
        in_specs=[SMEM_SPEC] + [VMEM_SPEC] * 11,
        out_specs=(VMEM_SPEC,) * 2,
        compiler_params=vmem_params(12),
        name="kv_far",
    )(place, gain, *weights, *near, *blocks)


def attend_kernel(
    place_ref, q_ref, acc_ref, stats_ref, past_ref, wo_ref, keep_ref, give_ref
):
    place = place_ref[0]
    first = place_ref[1] == 0
    head = lax.broadcasted_iota(jnp.int32, (SEG, LW), 1) // HD
    q, acc = q_ref[...], acc_ref[...]
    context = jnp.zeros((SEG, LW), F32)
    for h in range(LW // HD):
        qh = jnp.where(head == h, q, jnp.zeros_like(q))
        old = lax.dot_general(qh, past_ref[:, 0:LW], NT, preferred_element_type=F32)
        old = jnp.where(first, NEG_FILL, old * HD ** (-0.5))
        own_top = stats_ref[:, h : h + 1]
        top = jnp.maximum(own_top, jnp.max(old, axis=1, keepdims=True))
        old = jnp.exp(old - top)
        keep = jnp.exp(own_top - top)
        total = stats_ref[:, 4 + h : 5 + h] * keep + jnp.sum(old, axis=1, keepdims=True)
        mixed = acc * keep + jnp.dot(
            old.astype(BF16), past_ref[:, LW : 2 * LW], preferred_element_type=F32
        )
        context = jnp.where(head == h, mixed / total, context)
    context = context.astype(BF16)
    for flip, out_ref in ((1, give_ref), (0, keep_ref)):
        for d in range(4):
            start = pl.multiple_of(target_of(place, d, flip) * LW, LW)
            out_ref[d] = jnp.dot(
                context, wo_ref[:, pl.ds(start, LW)], preferred_element_type=F32
            ).astype(out_ref.dtype)


def attend(place, q, acc, stats, past, wo):
    return pl.pallas_call(
        attend_kernel,
        out_shape=(
            jax.ShapeDtypeStruct((4, SEG, LW), F32),
            jax.ShapeDtypeStruct((4, SEG, LW), BF16),
        ),
        in_specs=[SMEM_SPEC] + [VMEM_SPEC] * 5,
        out_specs=(VMEM_SPEC,) * 2,
        compiler_params=vmem_params(12),
        name="attend",
    )(place, q, acc, stats, past, wo)


def pair_kernel(keep_ref, got_ref, mine_ref, *out_refs):
    mine_ref[...] = keep_ref[0] + got_ref[0].astype(F32)
    for d in (1, 2, 3):
        out_refs[d - 1][...] = (keep_ref[d] + got_ref[d].astype(F32)).astype(BF16)


def pair(keep, got):
    shape = keep.shape[1:]
    return pl.pallas_call(
        pair_kernel,
        out_shape=(jax.ShapeDtypeStruct(shape, F32),) + (jax.ShapeDtypeStruct(shape, BF16),) * 3,
        in_specs=[VMEM_SPEC] * 2,
        out_specs=(VMEM_SPEC,) * 4,
        compiler_params=vmem_params(3),
        name="pair",
    )(keep, got)


def split_square(square):
    high = square.astype(BF16)
    low = (square - high.astype(F32)).astype(BF16)
    lane = lax.broadcasted_iota(jnp.int32, (square.shape[0], 128), 1)
    return jnp.where(
        lane == 0, high.astype(F32), jnp.where(lane == 1, low.astype(F32), 0.0)
    )


def project_kernel(
    place_ref, gain_ref, x_ref, a0_ref, a1_ref, a2_ref, a3_ref, ph_ref, pm_ref, pt_ref,
    hidden_ref, keep_ref, give_ref, part_ref,
):
    place = place_ref[0]
    attention = a0_ref[...]
    for ref in (a1_ref, a2_ref, a3_ref):
        attention = attention + ref[...].astype(F32)
    summed = x_ref[...].astype(F32) + attention
    hidden_ref[...] = summed.astype(BF16)
    square = jnp.sum(summed * summed, axis=1, keepdims=True)
    scaled = (summed * gain_ref[pl.ds(place, 1), :]).astype(BF16)
    part_ref[:, 0:P0] = jnp.dot(scaled, ph_ref[...], preferred_element_type=F32)
    part_ref[:, P0 : P0 + P1] = jnp.dot(scaled, pm_ref[...], preferred_element_type=F32)
    part_ref[:, P0 + P1 : BAND] = jnp.dot(scaled, pt_ref[...], preferred_element_type=F32)
    part_ref[:, BAND:WIDE] = split_square(square)
    for d in range(4):
        rows = pl.ds(pl.multiple_of(target_of(place, d, 1) * TOK, TOK), TOK)
        give_ref[d] = part_ref[rows, :].astype(BF16)
        rows = pl.ds(pl.multiple_of(target_of(place, d, 0) * TOK, TOK), TOK)
        keep_ref[d] = part_ref[rows, :]


def project(place, gain, x, parts, ph, pm, pt):
    return pl.pallas_call(
        project_kernel,
        out_shape=(
            jax.ShapeDtypeStruct((SEG, LW), BF16),
            jax.ShapeDtypeStruct((4, TOK, WIDE), F32),
            jax.ShapeDtypeStruct((4, TOK, WIDE), BF16),
        ),
        in_specs=[SMEM_SPEC] + [VMEM_SPEC] * 9,
        out_specs=(VMEM_SPEC,) * 3,
        scratch_shapes=[pltpu.VMEM((SEG, WIDE), F32)],
        compiler_params=vmem_params(12),
        name="project",
    )(place, gain, x, *parts, ph, pm, pt)


def pair_band_kernel(keep_ref, got_ref, mine_ref, *out_refs):
    for d in range(4):
        band = keep_ref[d, :, 0:BAND] + got_ref[d, :, 0:BAND].astype(F32)
        tail = keep_ref[d, :, BAND:WIDE] + got_ref[d, :, BAND:WIDE].astype(F32)
        if d == 0:
            mine_ref[:, 0:BAND] = band
            mine_ref[:, BAND:WIDE] = tail
        else:
            square = tail[:, 0:1] + tail[:, 1:2]
            out_refs[d - 1][:, 0:BAND] = band.astype(BF16)
            out_refs[d - 1][:, BAND:WIDE] = split_square(square).astype(BF16)


def pair_band(keep, got):
    shape = keep.shape[1:]
    return pl.pallas_call(
        pair_band_kernel,
        out_shape=(jax.ShapeDtypeStruct(shape, F32),) + (jax.ShapeDtypeStruct(shape, BF16),) * 3,
        in_specs=[VMEM_SPEC] * 2,
        out_specs=(VMEM_SPEC,) * 4,
        compiler_params=vmem_params(3),
        name="pair_band",
    )(keep, got)


def finish_band_kernel(place_ref, info_ref, a0_ref, a1_ref, a2_ref, a3_ref, out_ref):
    total = a0_ref[...]
    for ref in (a1_ref, a2_ref, a3_ref):
        total = total + ref[...].astype(F32)
    square = total[:, BAND : BAND + 1] + total[:, BAND + 1 : BAND + 2]
    out_ref[:, 0:BAND] = (total[:, 0:BAND] * lax.rsqrt(square / D + 1e-06)).astype(BF16)
    out_ref[:, BAND:WIDE] = info_ref[pl.ds(pl.multiple_of(place_ref[0] * TOK, TOK), TOK), :]


def finish_band(place, info, parts):
    return pl.pallas_call(
        finish_band_kernel,
        out_shape=jax.ShapeDtypeStruct((TOK, WIDE), BF16),
        in_specs=[SMEM_SPEC] + [VMEM_SPEC] * 5,
        out_specs=VMEM_SPEC,
        compiler_params=vmem_params(3),
        name="finish_band",
    )(place, info, *parts)


def target_info(targets):
    band = (targets >= V0).astype(jnp.int32) + (targets >= V0 + V1).astype(jnp.int32)
    code, row = jnp.zeros_like(targets), jnp.zeros_like(targets)
    for b, (first, rows) in enumerate(((0, HEAD_ROWS), (V0, MID_ROWS), (V0 + V1, TAIL_ROWS))):
        word = jnp.maximum(targets - first, 0)
        shard, within = word // rows, word % rows
        there, place = shard // N_CTX, shard % N_CTX
        code = jnp.where(band == b, 8 * b + there // 2 * 2 + place // 16, code)
        row = jnp.where(band == b, (place % 16 * 2 + there % 2) * rows + within, row)
    columns = jnp.stack([code, row // 256, row % 256], 1)
    return jnp.pad(columns, ((0, 0), (0, 125))).astype(BF16)


def turn_kernel(place_ref, clus_ref, *refs):
    blocks = refs[:8]
    flip_ref, cl_ref, goal_ref, rows_ref = refs[8:]
    y, half = place_ref[0] // 2, place_ref[1] // 16
    for j, ref in enumerate(blocks):
        src = lax.rem(y - j // 2 + 4, 4) + 4 * ((half + j) % 2)
        rows_ref[pl.ds(pl.multiple_of(src * TOK, TOK), TOK), :] = ref[...]
    flip_ref[...] = rows_ref[...].T
    cl_ref[...] = jnp.dot(clus_ref[...], flip_ref[0:P0, :], preferred_element_type=F32)
    info = flip_ref[BAND : BAND + 16, :].astype(F32)
    code = info[0:1].astype(jnp.int32)
    row = (info[1:2] * 256.0 + info[2:3]).astype(jnp.int32)
    goals = [jnp.where(code == 8 * b + 2 * y + half, row, -(1 << 24)) for b in range(3)]
    kind = (code >= 8).astype(jnp.int32) + (code >= 16).astype(jnp.int32)
    goal_ref[...] = jnp.concatenate(goals + [kind] * 5, 0)


def turned(place, clusters, blocks):
    return pl.pallas_call(
        turn_kernel,
        out_shape=(
            jax.ShapeDtypeStruct((WIDE, SEG), BF16),
            jax.ShapeDtypeStruct((2, SEG), F32),
            jax.ShapeDtypeStruct((8, SEG), jnp.int32),
        ),
        in_specs=[SMEM_SPEC] + [VMEM_SPEC] * 9,
        out_specs=(VMEM_SPEC,) * 3,
        scratch_shapes=[pltpu.VMEM((SEG, WIDE), BF16)],
        compiler_params=vmem_params(6),
        name="turned",
    )(place, clusters, *blocks)


def unpack_kernel(table_ref, head_ref, mid_ref, tail_ref, sem):
    def one(s, carry):
        for j in range(P0 // 256):
            to = pl.ds(pl.multiple_of(s * HEAD_ROWS, 8), HEAD_ROWS)
            pltpu.make_async_copy(
                table_ref.at[s, pl.ds(j * HEAD_ROWS, HEAD_ROWS), :],
                head_ref.at[to, pl.ds(j * 256, 256)], sem.at[0],
            ).start()
        for j in range(P1 // 256):
            to = pl.ds(pl.multiple_of(s * MID_ROWS, 8), MID_ROWS)
            pltpu.make_async_copy(
                table_ref.at[s, pl.ds(PACK_HEAD + j * MID_ROWS, MID_ROWS), :],
                mid_ref.at[to, pl.ds(j * 256, 256)], sem.at[1],
            ).start()
        for j, (offset, rows) in enumerate(((0, TAIL_LEFT), (TAIL_LEFT, TAIL_RIGHT))):
            to = pl.ds(pl.multiple_of(s * TAIL_ROWS + offset, 8), rows)
            pltpu.make_async_copy(
                table_ref.at[s, pl.ds(PACK_HEAD + PACK_MID, rows), pl.ds(j * 128, 128)],
                tail_ref.at[to, :], sem.at[2],
            ).start()
        return carry

    lax.fori_loop(0, N_CTX, one, 0)
    for k, ref in enumerate((head_ref, mid_ref, tail_ref)):
        pltpu.make_async_copy(ref, ref, sem.at[k]).wait()


def unpacked(table):
    return pl.pallas_call(
        unpack_kernel,
        out_shape=(
            jax.ShapeDtypeStruct((HEAD_ROWS * N_CTX, P0), BF16),
            jax.ShapeDtypeStruct((MID_ROWS * N_CTX, P1), BF16),
            jax.ShapeDtypeStruct((TAIL_ROWS * N_CTX, P2), BF16),
        ),
        in_specs=[ANY_SPEC],
        out_specs=(VMEM_SPEC,) * 3,
        scratch_shapes=[pltpu.SemaphoreType.DMA((3,))],
        compiler_params=vmem_params(40),
        name="unpacked",
    )(table)


LOG2_E = 1.4426950408889634
LANES = 2


def fold(words_ref, flip_ref, even_ref, odd_ref, first, width, total, goal, rows):
    near = goal - lax.broadcasted_iota(jnp.int32, (8, SEG), 0)
    flip = flip_ref.at[first : first + width, :]
    count = total // rows

    def load(i, store_ref):
        start = pl.multiple_of(i * rows, rows)
        logits = jnp.dot(
            words_ref[pl.ds(start, rows), :], flip[...], preferred_element_type=F32
        )
        store_ref[0:rows, :] = logits
        return jnp.max(logits.reshape(rows // 8, 8, SEG), axis=0)

    def use(i, store_ref, highest, state):
        top, acc, pick = state
        new_top = jnp.maximum(top, highest)
        shift = new_top * LOG2_E
        sums = [acc * jnp.exp2(top * LOG2_E - shift)] + [jnp.zeros((8, SEG), F32)] * (LANES - 1)
        picks = [pick] + [jnp.zeros((8, SEG), F32)] * (LANES - 1)
        here = near - i * rows
        for r in range(rows // 8):
            part = store_ref[8 * r : 8 * r + 8, :]
            k = r % LANES
            sums[k] = sums[k] + jnp.exp2(part * LOG2_E - shift)
            picks[k] = jnp.where(here == 8 * r, part, picks[k])
        return new_top, sum(sums[1:], sums[0]), sum(picks[1:], picks[0])

    def step(i, carry):
        state, highest = carry
        following = load(2 * i + 1, odd_ref)
        state = use(2 * i, even_ref, highest, state)
        highest = load(jnp.minimum(2 * i + 2, count - 1), even_ref)
        state = use(2 * i + 1, odd_ref, following, state)
        return state, highest

    empty = (
        jnp.full((8, SEG), NEG_FILL, F32),
        jnp.zeros((8, SEG), F32),
        jnp.zeros((8, SEG), F32),
    )
    (top, acc, pick), _ = lax.fori_loop(0, count // 2, step, (empty, load(0, even_ref)))
    highest = jnp.max(top, axis=0, keepdims=True)
    total_exp = jnp.sum(acc * jnp.exp(top - highest), axis=0, keepdims=True)
    return highest, total_exp, jnp.sum(pick, axis=0, keepdims=True)


def words_kernel(goal_ref, flip_ref, head_ref, mid_ref, tail_ref, out_ref, even_ref, odd_ref):
    refs = (flip_ref, even_ref, odd_ref)
    n0, n1, n2 = HEAD_ROWS * N_CTX, MID_ROWS * N_CTX, TAIL_ROWS * N_CTX
    m = fold(mid_ref, *refs, P0, P1, n1, goal_ref[1:2, :], 640)
    t = fold(tail_ref, *refs, P0 + P1, P2, n2, goal_ref[2:3, :], 816)
    h = fold(head_ref, *refs, 0, P0, n0, goal_ref[0:1, :], 640)
    out_ref[...] = jnp.concatenate(
        [h[0], h[1], m[0], m[1], t[0], t[1], h[2] + m[2] + t[2], jnp.zeros((1, SEG), F32)], 0
    )


def words(goals, flip, tables):
    return pl.pallas_call(
        words_kernel,
        out_shape=jax.ShapeDtypeStruct((8, SEG), F32),
        in_specs=[VMEM_SPEC] * 5,
        out_specs=VMEM_SPEC,
        scratch_shapes=[pltpu.VMEM((816, SEG), F32), pltpu.VMEM((816, SEG), F32)],
        compiler_params=vmem_params(6),
        name="words",
    )(goals, flip, *tables)


def join(one, other):
    rows = []
    for b in range(3):
        top = jnp.maximum(one[2 * b : 2 * b + 1], other[2 * b : 2 * b + 1])
        rows += [
            top,
            one[2 * b + 1 : 2 * b + 2] * jnp.exp(one[2 * b : 2 * b + 1] - top)
            + other[2 * b + 1 : 2 * b + 2] * jnp.exp(other[2 * b : 2 * b + 1] - top),
        ]
    return jnp.concatenate(rows + [one[6:7] + other[6:7], jnp.zeros((1, SEG), F32)], 0)


def join_kernel(a_ref, b_ref, out_ref):
    out_ref[...] = join(a_ref[...], b_ref[...])


def loss_kernel(place_ref, goal_ref, cl_ref, a_ref, b_ref, c_ref, d_ref, out_ref):
    stats = join(join(a_ref[...], b_ref[...]), join(c_ref[...], d_ref[...]))
    kind = goal_ref[3:4, :]
    c0, c1 = cl_ref[0:1, :], cl_ref[1:2, :]
    word_total = stats[0:1] + jnp.log(stats[1:2])
    top = jnp.maximum(word_total, jnp.maximum(c0, c1))
    head_total = top + jnp.log(
        jnp.exp(word_total - top) + jnp.exp(c0 - top) + jnp.exp(c1 - top)
    )
    mid_total = stats[2:3] + jnp.log(stats[3:4])
    tail_total = stats[4:5] + jnp.log(stats[5:6])
    pick = stats[6:7]
    losses = jnp.where(
        kind == 0,
        head_total - pick,
        jnp.where(
            kind == 1,
            head_total - c0 + mid_total - pick,
            head_total - c1 + tail_total - pick,
        ),
    )
    losses = jnp.where(place_ref[1] < 16, losses[:, 0:128], losses[:, 128:256])
    out_ref[...] = jnp.broadcast_to(losses, (8, 128))


def order_kernel(place_ref, mine_ref, other_ref, out_ref):
    core = place_ref[0] % 2
    mine, other = mine_ref[...], other_ref[...]
    lane = lax.broadcasted_iota(jnp.int32, (8, SEG), 1) // TOK
    out = jnp.zeros((8, SEG), F32)
    for c in range(2):
        half = jnp.where(core == c, mine, other)
        both = jnp.concatenate([half, half], 1)
        for y in range(4):
            shift = (y + c) * TOK
            moved = pltpu.roll(both, shift, 1) if shift else both
            out = jnp.where(lane == 2 * y + c, moved, out)
    out_ref[...] = out[0:1]


def ordered(place, mine, other):
    return pl.pallas_call(
        order_kernel,
        out_shape=jax.ShapeDtypeStruct((1, SEG), F32),
        in_specs=[SMEM_SPEC] + [VMEM_SPEC] * 2,
        out_specs=VMEM_SPEC,
        compiler_params=vmem_params(1),
        name="ordered",
    )(place, mine, other)


def joined(one, other):
    return pl.pallas_call(
        join_kernel,
        out_shape=jax.ShapeDtypeStruct((8, SEG), F32),
        in_specs=[VMEM_SPEC] * 2,
        out_specs=VMEM_SPEC,
        compiler_params=vmem_params(1),
        name="joined",
    )(one, other)


def loss(place, goals, cl, stats):
    return pl.pallas_call(
        loss_kernel,
        out_shape=jax.ShapeDtypeStruct((8, 128), F32),
        in_specs=[SMEM_SPEC] + [VMEM_SPEC] * 6,
        out_specs=VMEM_SPEC,
        compiler_params=vmem_params(1),
        name="loss",
    )(place, goals, cl, *stats)


def pack_kernel(head_ref, mid_ref, tail_ref, out_ref, sem):
    copies = []
    for j in range(P0 // 256):
        copies.append((head_ref.at[:, pl.ds(j * 256, 256)], j * HEAD_ROWS, HEAD_ROWS, 0, 256))
    for j in range(P1 // 256):
        start = PACK_HEAD + j * MID_ROWS
        copies.append((mid_ref.at[:, pl.ds(j * 256, 256)], start, MID_ROWS, 0, 256))
    start = PACK_HEAD + PACK_MID
    copies.append((tail_ref.at[pl.ds(0, TAIL_LEFT), :], start, TAIL_LEFT, 0, 128))
    copies.append((tail_ref.at[pl.ds(TAIL_LEFT, TAIL_RIGHT), :], start, TAIL_RIGHT, 128, 128))
    under = TAIL_LEFT - TAIL_RIGHT
    copies.append((tail_ref.at[pl.ds(0, under), :], start + TAIL_RIGHT, under, 128, 128))
    moves = [
        pltpu.make_async_copy(
            source, out_ref.at[pl.ds(row, rows), pl.ds(col, cols)], sem.at[i]
        )
        for i, (source, row, rows, col, cols) in enumerate(copies)
    ]
    for move in moves:
        move.start()
    for move in moves:
        move.wait()


def packed_tables(table_head, table_middle, table_tail):
    return pl.pallas_call(
        pack_kernel,
        out_shape=jax.ShapeDtypeStruct((PACK_ROWS, 256), BF16),
        in_specs=[ANY_SPEC] * 3,
        out_specs=ANY_SPEC,
        scratch_shapes=[pltpu.SemaphoreType.DMA((P0 // 256 + P1 // 256 + 3,))],
        compiler_params=vmem_params(1),
        name="packed",
    )(table_head, table_middle, table_tail)


def layer(
    hidden_in, norm_gain, w_query, w_key, w_value, w_out, head_gain,
    proj_head, proj_middle, proj_tail, table_head, table_middle, table_tail, clusters, targets,
):
    tp_rank = lax.axis_index(TP)
    ctx_rank = lax.axis_index(CTX)
    place = jnp.stack([tp_rank, ctx_rank]).astype(jnp.int32)
    info = target_info(targets)
    gain = norm_gain.reshape(N_TP, LW)
    weights = (w_query, w_key, w_value)
    blocks = {}
    blocks[0, 1] = to_partner(hidden_in)
    for d in (1, 3, 2):
        blocks[d, 0] = to_y(hidden_in, d)
    blocks[0, 1], *tables = lax.optimization_barrier(
        (blocks[0, 1], table_head, table_middle, table_tail)
    )
    table = lax.all_gather(packed_tables(*tables), ("xl", "z", "core"))
    for d in (1, 3, 2):
        blocks[d, 1] = to_partner(blocks[d, 0])
    near = qkv_near(place, gain, weights, (hidden_in, blocks[0, 1]))
    far = [blocks[e] for e in FAR]
    now, scale = kv_far(place, gain, weights[1:], near, far)
    past = lax.ppermute(now, CTX, [(i, i + 1) for i in range(N_CTX - 1)])
    q, acc, stats = own_attention(place, gain, w_query, near[0], scale, now, far)
    keep, give = attend(place, q, acc, stats, past, w_out)
    mine, *others = pair(keep, to_partner(give))
    parts = [mine] + [to_y(o, d) for o, d in zip(others, (1, 2, 3))]
    hidden_out, keep, give = project(
        place, head_gain.reshape(N_TP, LW), hidden_in, parts, proj_head, proj_middle, proj_tail
    )
    mine, *others = pair_band(keep, to_partner(give))
    parts = [mine] + [to_y(o, d) for o, d in zip(others, (1, 2, 3))]
    band = finish_band(place, info, parts)
    band_x = to_mate(band)
    tables = unpacked(table)
    bands = [band, band_x]
    for d in (1, 2, 3):
        bands.append(to_y(band, d))
        bands.append(to_y(band_x, d))
    *bands, first, second, third = lax.optimization_barrier((*bands, *tables))
    flip, cl, goals = turned(place, clusters, bands)
    stats = words(goals, flip, (first, second, third))
    stats = joined(stats, to_mate(stats))
    done = loss(place, goals, cl, from_y(stats))
    losses = ordered(place, done, to_partner(done)).reshape(SEG)
    return (hidden_out, losses)


def solution(mesh):
    fine = Mesh(mesh.devices.reshape(2, 2, 8, 4, 2), CTX + TP)
    placed = (
        P(CTX, TP),
        P(),
        P(None, TP),
        P(None, TP),
        P(None, TP),
        P(TP, None),
        P(),
        P(TP, None),
        P(TP, None),
        P(TP, None),
        P(TP + CTX, None),
        P(TP + CTX, None),
        P(TP + CTX, None),
        P(),
        P(CTX),
    )
    return jax.shard_map(
        layer, mesh=fine, in_specs=placed, out_specs=(P(CTX, TP), P(CTX)), check_vma=False
    )
```
